32 devices in a mesh: dev: 32 (over z, y, x, core).
Axes of the slice: x: 2, y: 2, z: 4, core: 2. Of those that a mesh axis runs over, the one named last changes fastest.
Arguments:
- images: bfloat16 [64, 196, 512], P('dev'), may hold values from -6 to 6
- cotangent: float32 [64, 196, 512], P('dev'), may hold values from -6 to 6
- image_counts: int32 [32], P('dev'), may hold values from 0 to 2, as said below
- relative_index: int32 [49, 49], replicated, may hold values from 0 to 168
- region_labels: int32 [196], replicated, may hold values from 0 to 3
- gain_first: bfloat16 [512], P('dev'), may hold values from 0.5 to 1.5
- shift_first: bfloat16 [512], P('dev'), may hold values from -3 to 3
- attend_weight: bfloat16 [786432], P('dev'), may hold values from -0.25 to 0.25
- query_bias: bfloat16 [512], P('dev'), may hold values from -4 to 4
- value_bias: bfloat16 [512], P('dev'), may hold values from -3 to 3
- position_table: bfloat16 [2720], P('dev'), may hold values from -4 to 300
- output_weight: bfloat16 [262144], P('dev'), may hold values from -0.5 to 0.5
- output_bias: bfloat16 [512], P('dev'), may hold values from -3 to 3
- gain_second: bfloat16 [512], P('dev'), may hold values from 0.5 to 1.5
- shift_second: bfloat16 [512], P('dev'), may hold values from -3 to 3
- expand_weight: bfloat16 [1048576], P('dev'), may hold values from -0.25 to 0.25
- expand_bias: bfloat16 [2048], P('dev'), may hold values from -3 to 3
- reduce_weight: bfloat16 [1048576], P('dev'), may hold values from -0.125 to 0.125
- reduce_bias: bfloat16 [512], P('dev'), may hold values from -3 to 3
Outputs:
- block_output: float32 [64, 196, 512], P('dev')
- input_gradient: float32 [64, 196, 512], P('dev')
- gain_first_gradient: float32 [512], P('dev')
- shift_first_gradient: float32 [512], P('dev')
- attend_weight_gradient: float32 [786432], P('dev')
- query_bias_gradient: float32 [512], P('dev')
- value_bias_gradient: float32 [512], P('dev')
- position_table_gradient: float32 [2720], P('dev')
- output_weight_gradient: float32 [262144], P('dev')
- output_bias_gradient: float32 [512], P('dev')
- gain_second_gradient: float32 [512], P('dev')
- shift_second_gradient: float32 [512], P('dev')
- expand_weight_gradient: float32 [1048576], P('dev')
- expand_bias_gradient: float32 [2048], P('dev')
- reduce_weight_gradient: float32 [1048576], P('dev')
- reduce_bias_gradient: float32 [512], P('dev')
The draws below stay inside these ranges and needn't reach their ends.
Inputs may be any that keep to these rules, and one draw needn't show every extreme that they name: `image_counts`: number of live image slots of each device; some device holds 2 in every draw.
All inputs are finite; a program needn't handle non-finite values.
Results may differ from the reference program's by a relative error of at most 0.012.
Values may be sent and summed in bfloat16 or wider, within the bound.
No kernel may reach another device: no remote copies, remote signals or barrier semaphores. Data moves between devices by JAX's collectives and lax.ppermute only.
A program may use at most 128 MiB of HBM per device.

```python
import jax
import jax.numpy as jnp
from jax import lax

D = 512
HEADS = 16
HEAD_DIM = 32
FF = 2048
WIN = 7
SIDE = 14
SHIFT = 3
IMG_CAP = 2
TOK_IMG = 196
TABLE_ROWS = 169
SLOTS = 64
VEC_PAD = 512
FF_PAD = 2048
TAB_PAD = 2720
DEVICES = 32


def draw_image_counts(key, part):
    counts = jax.random.randint(key, (DEVICES,), 0, IMG_CAP + 1, dtype=jnp.int32)
    chosen = jax.random.randint(jax.random.fold_in(key, 7), (), 0, DEVICES, dtype=jnp.int32)
    return jnp.where(jnp.arange(DEVICES, dtype=jnp.int32) == chosen, IMG_CAP, counts).astype(jnp.int32)


def draw_position_table(key, part):
    value_key = jax.random.fold_in(key, 11)
    return jnp.clip(jax.random.normal(value_key, (TAB_PAD,), jnp.float32), -4.0, 4.0).astype(jnp.bfloat16)


def touch_ends(result, key, smallest, largest):
    longest = result.shape.index(max(result.shape))
    spots = []
    for shift in (0, 1):
        where = [jax.random.randint(jax.random.fold_in(key, axis), (), 0, length) for axis, length in enumerate(result.shape)]
        where[longest] = (where[longest] + shift) % result.shape[longest]
        spots.append(tuple(where))
    return result.at[spots[0]].set(smallest).at[spots[1]].set(largest)


def block_scale(key, extent, pieces, least, high):
    def one(dim, blocks):
        heights = jax.random.uniform(jax.random.fold_in(jax.random.fold_in(key, 6), dim), (blocks,), jnp.float32, least / len(pieces), high / len(pieces))
        return jnp.repeat(jnp.exp(heights), extent[dim] // blocks).reshape((-1,) + (1,) * (len(extent) - dim - 1))

    factor_of = one(*pieces[0])
    for cut in pieces[1:]:
        factor_of = factor_of * one(*cut)
    return factor_of


def gaussian(rng, shape, deviation, most, split=(), kind=jnp.bfloat16):
    level = block_scale(rng, shape, split, -0.22, 0.18) if split else 1.0
    drawn = jax.random.normal(rng, shape, jnp.float32) * deviation * level
    return jnp.minimum(jnp.maximum(drawn, -most), most).astype(kind)


def setup_inputs(seed: int = 0) -> dict:
    keys = jax.random.split(jax.random.key(seed), 20)
    return {
        "images": gaussian(keys[0], (SLOTS, TOK_IMG, D), 1.0, 6.0, ((0, 32),)),
        "cotangent": gaussian(keys[1], (SLOTS, TOK_IMG, D), 1.0, 6.0, ((0, 32),), jnp.float32),
        "image_counts": draw_image_counts(jax.random.fold_in(keys[19], 71), 0),
        "relative_index": touch_ends(jax.random.randint(keys[3], (WIN * WIN, WIN * WIN), 0, TABLE_ROWS), jax.random.fold_in(keys[3], 1), 0, TABLE_ROWS - 1).astype(jnp.int32),
        "region_labels": touch_ends(jax.random.randint(keys[4], (TOK_IMG,), 0, 4), jax.random.fold_in(keys[4], 1), 0, 3).astype(jnp.int32),
        "gain_first": jnp.clip(1.0 + 0.1 * jax.random.normal(keys[5], (VEC_PAD,), jnp.float32), 0.5, 1.5).astype(jnp.bfloat16),
        "shift_first": gaussian(keys[6], (VEC_PAD,), 0.5, 3.0, ((0, 32),)),
        "attend_weight": gaussian(keys[7], (3 * D * D,), D ** -0.5, 0.25, ((0, 32),)),
        "query_bias": gaussian(keys[8], (VEC_PAD,), 1.0, 4.0, ((0, 32),)),
        "value_bias": gaussian(keys[9], (VEC_PAD,), 0.5, 3.0, ((0, 32),)),
        "position_table": draw_position_table(jax.random.fold_in(keys[19], 71), 0),
        "output_weight": gaussian(keys[11], (D * D,), (D // 4) ** -0.5, 0.5, ((0, 32),)),
        "output_bias": gaussian(keys[12], (VEC_PAD,), 0.5, 3.0, ((0, 32),)),
        "gain_second": jnp.clip(1.0 + 0.1 * jax.random.normal(keys[13], (VEC_PAD,), jnp.float32), 0.5, 1.5).astype(jnp.bfloat16),
        "shift_second": gaussian(keys[14], (VEC_PAD,), 0.5, 3.0, ((0, 32),)),
        "expand_weight": gaussian(keys[15], (D * FF,), D ** -0.5, 0.25, ((0, 32),)),
        "expand_bias": gaussian(keys[16], (FF_PAD,), 0.5, 3.0, ((0, 32),)),
        "reduce_weight": gaussian(keys[17], (FF * D,), FF ** -0.5, 0.125, ((0, 32),)),
        "reduce_bias": gaussian(keys[18], (VEC_PAD,), 0.5, 3.0, ((0, 32),)),
    }


EPS = 1e-05
NEG = -1e+30
INV_ROOT_TWO = 0.7071067811865476
INV_ROOT_TWO_PI = 0.3989422804014327

def layer_norm(inputs, gain_vec, shift_vec):
    centered = inputs - lax.optimization_barrier(jnp.mean(inputs, -1, keepdims=True))
    inv_std = lax.rsqrt(lax.optimization_barrier(jnp.mean(centered * centered, -1, keepdims=True)) + EPS)
    normed = centered * inv_std
    return (normed, inv_std, normed * gain_vec + shift_vec)

def norm_back(grad_normed, normed, inv_std):
    first = lax.optimization_barrier(jnp.mean(grad_normed, -1, keepdims=True))
    second = lax.optimization_barrier(jnp.mean(grad_normed * normed, -1, keepdims=True))
    return inv_std * (grad_normed - first - normed * second)

def gelu_value(inputs):
    return 0.5 * inputs * (1.0 + lax.erf(inputs * INV_ROOT_TWO))

def gelu_slope(inputs):
    return 0.5 * (1.0 + lax.erf(inputs * INV_ROOT_TWO)) + inputs * jnp.exp(-0.5 * inputs * inputs) * INV_ROOT_TWO_PI

def to_windows(tokens_in):
    channels = tokens_in.shape[-1]
    blocks = SIDE // WIN
    grid_cells = jnp.roll(tokens_in.reshape(SIDE, SIDE, channels), (-SHIFT, -SHIFT), (0, 1))
    grid_cells = grid_cells.reshape(blocks, WIN, blocks, WIN, channels).transpose(0, 2, 1, 3, 4)
    return grid_cells.reshape(blocks * blocks, WIN * WIN, channels)

def from_windows(windows):
    channels = windows.shape[-1]
    blocks = SIDE // WIN
    grid_cells = windows.reshape(blocks, blocks, WIN, WIN, channels).transpose(0, 2, 1, 3, 4)
    grid_cells = jnp.roll(grid_cells.reshape(SIDE, SIDE, channels), (SHIFT, SHIFT), (0, 1))
    return grid_cells.reshape(SIDE * SIDE, channels)

def region_mask(region_labels):
    blocks = SIDE // WIN
    labels = region_labels.reshape(blocks, WIN, blocks, WIN).transpose(0, 2, 1, 3).reshape(blocks * blocks, WIN * WIN)
    return labels[:, :, None] == labels[:, None, :]

def index_table(relative_index):
    return (relative_index[:, :, None] == jnp.arange(TABLE_ROWS, dtype=jnp.int32)).astype(jnp.float32)

def unpack(flat_params):
    return {'gain_a': flat_params[0][:D].astype(jnp.float32), 'shift_a': flat_params[1][:D].astype(jnp.float32), 'attend': flat_params[2].reshape(D, 3 * D), 'query_bias': flat_params[3][:D].astype(jnp.float32), 'value_bias': flat_params[4][:D].astype(jnp.float32), 'table': flat_params[5][:TABLE_ROWS * HEADS].astype(jnp.float32).reshape(TABLE_ROWS, HEADS), 'out_w': flat_params[6].reshape(D, D), 'out_b': flat_params[7][:D].astype(jnp.float32), 'gain_b': flat_params[8][:D].astype(jnp.float32), 'shift_b': flat_params[9][:D].astype(jnp.float32), 'expand': flat_params[10].reshape(D, FF), 'expand_bias': flat_params[11][:FF].astype(jnp.float32), 'reduce': flat_params[12].reshape(FF, D), 'reduce_bias': flat_params[13][:D].astype(jnp.float32)}

def masked_scores(queries, key_rows, bias, allowed):
    raw = jnp.einsum('wihd,wjhd->whij', queries.astype(jnp.float32), key_rows.astype(jnp.float32))
    raw = raw + bias[None]
    return jnp.where(allowed[:, None], raw, NEG)

def forward_image(one_image, params, bias, allowed):
    inputs = one_image.astype(jnp.float32)
    normed_a, inv_std_a, mixed_a = layer_norm(inputs, params['gain_a'], params['shift_a'])
    windows = to_windows(mixed_a.astype(jnp.bfloat16))
    blocks = windows.shape[0]
    area = WIN * WIN
    projected = jnp.dot(windows.reshape(-1, D), params['attend'], preferred_element_type=jnp.float32)
    projected = projected.reshape(blocks, area, 3 * D)
    score_scale = HEAD_DIM ** (-0.5)
    queries = ((projected[..., :D] + params['query_bias']) * score_scale).astype(jnp.bfloat16)
    queries = queries.reshape(blocks, area, HEADS, HEAD_DIM)
    key_rows = projected[..., D:2 * D].astype(jnp.bfloat16).reshape(blocks, area, HEADS, HEAD_DIM)
    value_rows = (projected[..., 2 * D:] + params['value_bias']).astype(jnp.bfloat16)
    value_rows = value_rows.reshape(blocks, area, HEADS, HEAD_DIM)
    scores = masked_scores(queries, key_rows, bias, allowed)
    row_peak = lax.optimization_barrier(jnp.max(scores, -1, keepdims=True))
    row_total = lax.optimization_barrier(jnp.sum(jnp.exp(scores - row_peak), -1, keepdims=True))
    log_total = row_peak + jnp.log(row_total)
    attention = jnp.exp(scores - log_total).astype(jnp.bfloat16)
    mixed = jnp.einsum('whij,wjhd->wihd', attention.astype(jnp.float32), value_rows.astype(jnp.float32))
    attended = from_windows(mixed.astype(jnp.bfloat16).reshape(blocks, area, D))
    after_attention = inputs + jnp.dot(attended, params['out_w'], preferred_element_type=jnp.float32) + params['out_b']
    normed_b, inv_std_b, mixed_b = layer_norm(after_attention, params['gain_b'], params['shift_b'])
    hidden_in = mixed_b.astype(jnp.bfloat16)
    expanded = jnp.dot(hidden_in, params['expand'], preferred_element_type=jnp.float32) + params['expand_bias']
    activated = gelu_value(expanded).astype(jnp.bfloat16)
    output = after_attention + jnp.dot(activated, params['reduce'], preferred_element_type=jnp.float32) + params['reduce_bias']
    saved = (windows, queries, key_rows, value_rows, log_total, attended, normed_a, inv_std_a, normed_b, inv_std_b, hidden_in, expanded, activated)
    return (output, saved)

def backward_image(saved, cotan, params, bias, allowed, onehot):
    windows, queries, key_rows, value_rows, log_total, attended, normed_a, inv_std_a, normed_b, inv_std_b, hidden_in, expanded, activated = saved
    blocks = windows.shape[0]
    area = WIN * WIN
    cotan_half = cotan.astype(jnp.bfloat16)
    grad_reduce = jnp.dot(activated.T, cotan_half, preferred_element_type=jnp.float32)
    grad_reduce_bias = lax.optimization_barrier(jnp.sum(cotan, 0))
    grad_act = jnp.dot(cotan_half, params['reduce'].T, preferred_element_type=jnp.float32)
    grad_expanded = grad_act * gelu_slope(expanded)
    grad_exp_half = grad_expanded.astype(jnp.bfloat16)
    grad_expand = jnp.dot(hidden_in.T, grad_exp_half, preferred_element_type=jnp.float32)
    grad_expand_bias = lax.optimization_barrier(jnp.sum(grad_expanded, 0))
    grad_mixed_b = jnp.dot(grad_exp_half, params['expand'].T, preferred_element_type=jnp.float32)
    grad_gain_b = lax.optimization_barrier(jnp.sum(grad_mixed_b * normed_b, 0))
    grad_shift_b = lax.optimization_barrier(jnp.sum(grad_mixed_b, 0))
    grad_after = cotan + norm_back(grad_mixed_b * params['gain_b'], normed_b, inv_std_b)
    grad_after_half = grad_after.astype(jnp.bfloat16)
    grad_out_w = jnp.dot(attended.T, grad_after_half, preferred_element_type=jnp.float32)
    grad_out_b = lax.optimization_barrier(jnp.sum(grad_after, 0))
    grad_attended = jnp.dot(grad_after_half, params['out_w'].T, preferred_element_type=jnp.float32).astype(jnp.bfloat16)
    grad_mixed = to_windows(grad_attended).reshape(blocks, area, HEADS, HEAD_DIM)
    scores = masked_scores(queries, key_rows, bias, allowed)
    attention_full = jnp.exp(scores - log_total)
    attention = attention_full.astype(jnp.bfloat16)
    grad_values = jnp.einsum('whij,wihd->wjhd', attention.astype(jnp.float32), grad_mixed.astype(jnp.float32))
    grad_weights = jnp.einsum('wihd,wjhd->whij', grad_mixed.astype(jnp.float32), value_rows.astype(jnp.float32))
    grad_scores = attention_full * (grad_weights - lax.optimization_barrier(jnp.sum(attention_full * grad_weights, -1, keepdims=True)))
    grad_bias = lax.optimization_barrier(jnp.sum(grad_scores, 0))
    grad_table = jnp.einsum('ijt,hij->th', onehot, grad_bias, precision=lax.Precision.HIGHEST)
    grad_scores_half = grad_scores.astype(jnp.bfloat16).astype(jnp.float32)
    score_scale = HEAD_DIM ** (-0.5)
    grad_queries = jnp.einsum('whij,wjhd->wihd', grad_scores_half, key_rows.astype(jnp.float32)) * score_scale
    grad_keys = jnp.einsum('whij,wihd->wjhd', grad_scores_half, queries.astype(jnp.float32))
    grad_queries = grad_queries.reshape(blocks * area, D)
    grad_keys = grad_keys.reshape(blocks * area, D)
    grad_values = grad_values.reshape(blocks * area, D)
    grad_projected = jnp.concatenate([grad_queries, grad_keys, grad_values], -1).astype(jnp.bfloat16)
    grad_attend = jnp.dot(windows.reshape(-1, D).T, grad_projected, preferred_element_type=jnp.float32)
    grad_query_bias = lax.optimization_barrier(jnp.sum(grad_queries, 0))
    grad_value_bias = lax.optimization_barrier(jnp.sum(grad_values, 0))
    grad_windows = jnp.dot(grad_projected, params['attend'].T, preferred_element_type=jnp.float32)
    grad_mixed_a = from_windows(grad_windows.reshape(blocks, area, D))
    grad_gain_a = lax.optimization_barrier(jnp.sum(grad_mixed_a * normed_a, 0))
    grad_shift_a = lax.optimization_barrier(jnp.sum(grad_mixed_a, 0))
    grad_input = grad_after + norm_back(grad_mixed_a * params['gain_a'], normed_a, inv_std_a)
    grads = (grad_gain_a, grad_shift_a, grad_attend, grad_query_bias, grad_value_bias, grad_table, grad_out_w, grad_out_b, grad_gain_b, grad_shift_b, grad_expand, grad_expand_bias, grad_reduce, grad_reduce_bias)
    return (grad_input, grads)

def grad_shapes():
    return [(D,), (D,), (D, 3 * D), (D,), (D,), (TABLE_ROWS, HEADS), (D, D), (D,), (D,), (D,), (D, FF), (FF,), (FF, D), (D,)]

def reference(images, cotangent, image_counts, relative_index, region_labels, gain_first, shift_first, attend_weight, query_bias, value_bias, position_table, output_weight, output_bias, gain_second, shift_second, expand_weight, expand_bias, reduce_weight, reduce_bias):
    flat_params = (gain_first, shift_first, attend_weight, query_bias, value_bias, position_table, output_weight, output_bias, gain_second, shift_second, expand_weight, expand_bias, reduce_weight, reduce_bias)
    params = unpack(flat_params)
    allowed = region_mask(region_labels)
    onehot = index_table(relative_index)
    bias = jnp.einsum('ijt,th->hij', onehot, params['table'], precision=lax.Precision.HIGHEST)

    def live_work(operand):
        one_image, cotan = operand
        output, saved = forward_image(one_image, params, bias, allowed)
        grad_input, grads = backward_image(saved, cotan, params, bias, allowed, onehot)
        return (output, grad_input, grads)

    def dead_work(operand):
        zeros_rows = jnp.zeros((TOK_IMG, D), jnp.float32)
        grads = tuple((jnp.zeros(shape_one, jnp.float32) for shape_one in grad_shapes()))
        return (zeros_rows, zeros_rows, grads)

    def step_slot(carry, operand):
        one_image, cotan, slot_index = operand
        live = slot_index % IMG_CAP < image_counts[slot_index // IMG_CAP]
        output, grad_input, grads = lax.cond(live, live_work, dead_work, (one_image, cotan))
        carry = tuple((total + piece for total, piece in zip(carry, grads)))
        return (carry, (output, grad_input))
    init = tuple((jnp.zeros(shape_one, jnp.float32) for shape_one in grad_shapes()))
    slot_ids = jnp.arange(SLOTS, dtype=jnp.int32)
    totals, stacked = lax.scan(step_slot, init, (images, cotangent, slot_ids))
    padded = [jnp.pad(total.reshape(-1), (0, full.shape[0] - total.size)) for total, full in zip(totals, flat_params)]
    return (stacked[0], stacked[1], padded[0], padded[1], padded[2], padded[3], padded[4], padded[5], padded[6], padded[7], padded[8], padded[9], padded[10], padded[11], padded[12], padded[13])
```

```python
import functools

import jax
import jax.numpy as jnp
import numpy as np
from jax import lax
from jax.experimental import pallas as pl
from jax.experimental.pallas import tpu as pltpu
from jax.sharding import PartitionSpec as P

D = 512
HEADS = 16
HEAD_DIM = 32
FF = 2048
WIN = 7
SIDE = 14
SHIFT = 3
TOK = SIDE * SIDE
AREA = WIN * WIN
BLOCKS = (SIDE // WIN) ** 2
TABLE_ROWS = 169
ROWS = 208
WROWS = 64
GROUP = 4
GROUPS = HEADS // GROUP
GL = GROUP * HEAD_DIM
GS = GROUP * WROWS
CHUNK = 512

EPS = 1e-05
NEG = -1e30
INV_ROOT_TWO = 0.7071067811865476
INV_ROOT_TWO_PI = 0.3989422804014327
SCALE = HEAD_DIM ** (-0.5)
BF = jnp.bfloat16
F32 = jnp.float32


def window_matrix():
    side = SIDE // WIN
    out = np.zeros((BLOCKS * WROWS, ROWS), np.float32)
    for w in range(BLOCKS):
        for t in range(AREA):
            i = ((w // side) * WIN + t // WIN + SHIFT) % SIDE
            j = ((w % side) * WIN + t % WIN + SHIFT) % SIDE
            out[w * WROWS + t, i * SIDE + j] = 1.0
    return out


def axis_steps(mesh):
    devices = list(mesh.devices.flat)
    n = len(devices)
    try:
        places = np.array([tuple(d.coords) + (d.core_on_chip,) for d in devices])
        steps = []
        for column in range(places.shape[1]):
            values = places[:, column] - places[:, column].min()
            size = len(set(values.tolist()))
            if size > 1:
                stride = int(np.argmax(values != values[0]))
                if not np.array_equal((np.arange(n) // stride) % size, values):
                    raise ValueError("order")
                steps.append((stride, size))
        steps.sort(reverse=True)
        if int(np.prod([size for _, size in steps])) != n:
            raise ValueError("size")
    except (AttributeError, ValueError):
        steps, stride = [], 1
        while stride < n:
            size = 2 if (n // stride) % 2 == 0 else n // stride
            steps.insert(0, (stride, size))
            stride *= size
    return steps


class Exchange:
    def __init__(self, mesh):
        self.n = mesh.devices.size
        self.steps = axis_steps(mesh)
        self.dims = len(self.steps)
        self.sizes = tuple(size for _, size in self.steps)
        rest = sorted(range(self.dims - 1), key=lambda d: (-self.sizes[d], d))
        first = rest[:1]
        others = rest[1:]
        core = [self.dims - 1]
        self.orders = (first + others + core, first + others[::-1] + core)

    def digit(self, d):
        stride, size = self.steps[d]
        return (lax.axis_index("dev") // stride) % size

    def shift(self, x, d, k):
        stride, size = self.steps[d]
        pairs = []
        for i in range(self.n):
            p = (i // stride) % size
            pairs.append((i, i + ((p + k) % size - p) * stride))
        return lax.ppermute(x, "dev", pairs)

    def gather(self, shard, order):
        x = shard.reshape((1,) * self.dims + shard.shape)
        for d in self.orders[order]:
            size = self.sizes[d]
            pieces = [x] + [self.shift(x, d, k) for k in range(1, size)]
            p = self.digit(d)
            placed = [lax.select_n((p - j) % size, *pieces) if size > 2 else
                      jnp.where(p == j, pieces[0], pieces[1]) for j in range(size)]
            x = jnp.concatenate(placed, axis=d)
        return x.reshape((self.n * shard.shape[0],) + shard.shape[1:])

    def scatter_sum(self, full, order, kind):
        rows = full.shape[0] // self.n
        x = full.reshape(self.sizes + (rows,) + full.shape[1:])
        for d in self.orders[order][::-1]:
            size = self.sizes[d]
            p = self.digit(d)
            x = x.astype(kind)
            total = lax.dynamic_index_in_dim(x, p, d, keepdims=True).astype(F32)
            for k in range(1, size):
                piece = lax.dynamic_index_in_dim(x, (p + k) % size, d, keepdims=True)
                total = total + self.shift(piece, d, k).astype(F32)
            x = total
        return x.reshape((rows,) + full.shape[1:])


def nn(a, b):
    return lax.dot_general(a, b, (((1,), (0,)), ((), ())), preferred_element_type=F32)


def nt(a, b):
    return lax.dot_general(a, b, (((1,), (1,)), ((), ())), preferred_element_type=F32)


def tn(a, b):
    return lax.dot_general(a, b, (((0,), (0,)), ((), ())), preferred_element_type=F32)


def normed_of(x):
    centered = x - jnp.mean(x, -1, keepdims=True)
    inv = lax.rsqrt(jnp.mean(centered * centered, -1, keepdims=True) + EPS)
    return centered * inv, inv


def norm_back(grad, normed, inv):
    first = jnp.mean(grad, -1, keepdims=True)
    second = jnp.mean(grad * normed, -1, keepdims=True)
    return inv * (grad - first - normed * second)


def column_sum(x):
    return jnp.sum(x, 0, keepdims=True)


def load_rows(ref, scratch, slots):
    for s in range(slots):
        scratch[s * ROWS + TOK // 8 * 8 : (s + 1) * ROWS, :] = jnp.zeros(
            (ROWS - TOK // 8 * 8, D), F32
        )
        scratch[s * ROWS : s * ROWS + TOK, :] = ref[s].astype(F32)


def head_masks(kind):
    lane = lax.broadcasted_iota(jnp.int32, (1, GL), 1) // HEAD_DIM
    return [(lane == h).astype(F32).astype(kind) for h in range(GROUP)]


def spread(x, masks):
    return jnp.concatenate([x * m for m in masks], axis=0)


def diagonal(x, masks):
    total = x[:WROWS] * masks[0]
    for h in range(1, GROUP):
        total = total + x[h * WROWS : (h + 1) * WROWS] * masks[h]
    return total


def attend_kernel(slots, images, qk_w, vo_w, vecs, bias, allowed, cut, paste,
                  qkv_out, pt_out, att_out, h1_out, rows, mixed):
    load_rows(images, rows, slots)
    normed, _ = normed_of(rows[...])
    h1 = (normed * vecs[0:1, :] + vecs[1:2, :]).astype(BF)
    h1_out[...] = h1
    q = ((nn(h1, qk_w[:, :D]) + vecs[2:3, :]) * SCALE).astype(BF)
    k = nn(h1, qk_w[:, D:]).astype(BF)
    v = (nn(h1, vo_w[:, :D]) + vecs[3:4, :]).astype(BF)
    wide = BLOCKS * WROWS
    for s in range(slots):
        for place, part in enumerate((q, k, v)):
            qkv_out[s * wide : (s + 1) * wide, place * D : (place + 1) * D] = nn(
                cut[...], part[s * ROWS : (s + 1) * ROWS]
            ).astype(BF)
    half = head_masks(BF)
    full = head_masks(F32)

    def step(iw, carry):
        at = pl.ds(pl.multiple_of(iw * WROWS, WROWS), WROWS)
        ok = allowed[iw % BLOCKS] > 0.0
        ok = jnp.concatenate([ok.astype(F32)] * GROUP, axis=1) > 0.0
        for g in range(GROUPS):
            lanes = slice(g * GL, (g + 1) * GL)
            wide_lanes = slice(g * GS, (g + 1) * GS)
            qg = qkv_out[at, g * GL : (g + 1) * GL]
            kg = qkv_out[at, D + g * GL : D + (g + 1) * GL]
            vg = qkv_out[at, 2 * D + g * GL : 2 * D + (g + 1) * GL]
            s = nt(kg, spread(qg, half)) + bias[:, wide_lanes]
            s = jnp.where(ok, s, NEG)
            e = jnp.exp(s - jnp.max(s, 0, keepdims=True))
            p = e * (1.0 / jnp.sum(e, 0, keepdims=True))
            pt_out[iw, :, wide_lanes] = p
            mixed[at, lanes] = diagonal(tn(p.astype(BF), vg), full).astype(BF)
        return carry

    lax.fori_loop(0, slots * BLOCKS, step, 0)
    for s in range(slots):
        att_out[s * ROWS : (s + 1) * ROWS, :] = nn(
            paste[...], mixed[s * wide : (s + 1) * wide, :]
        ).astype(BF)


def mixer_kernel(slots, counts, images, cotangent, attended, vo_w, expand, reduce, vecs, ebias,
                 out, after_out, gatt_out, gow_out, ge_out, gr_out, small_out, geb_out,
                 rows, cot, after_s, total, gh2, h2_s, h2t_s):
    load_rows(images, rows, slots)
    load_rows(cotangent, cot, slots)
    live = [counts[0] > s for s in range(slots)]
    for s in range(slots):
        at = slice(s * ROWS, (s + 1) * ROWS)
        cot[at, :] = jnp.where(live[s], cot[at, :], 0.0)
    att = attended[...]
    out_w = vo_w[:, D:]
    after = rows[...] + nn(att, out_w) + vecs[0:1, :]
    after_s[...] = after
    normed, inv = normed_of(after)
    h2 = (normed * vecs[1:2, :] + vecs[2:3, :]).astype(BF)
    h2_s[...] = h2
    h2t_s[...] = h2.T
    total[...] = after + vecs[3:4, :]
    gh2[...] = jnp.zeros_like(gh2)

    def step(c, carry):
        at = pl.ds(pl.multiple_of(c * CHUNK, CHUNK), CHUNK)
        gb = cot[...].astype(BF)
        we = expand[:, at]
        wr = reduce[at, :]
        u = nn(h2_s[...], we) + ebias[:, at]
        cdf = 0.5 * (1.0 + lax.erf(u * INV_ROOT_TWO))
        slope = cdf + u * jnp.exp(-0.5 * u * u) * INV_ROOT_TWO_PI
        act = (u * cdf).astype(BF)
        total[...] += nn(act, wr)
        gr_out[at, :] = tn(act, gb).astype(BF)
        ge = nt(gb, wr) * slope
        geb_out[:, at] = column_sum(ge)
        geh = ge.astype(BF)
        ge_out[:, at] = nn(h2t_s[...], geh).astype(BF)
        gh2[...] += nt(geh, we)
        return carry

    lax.fori_loop(0, FF // CHUNK, step, 0)
    for s in range(slots):
        out[s] = jnp.where(live[s], total[s * ROWS : s * ROWS + TOK, :], 0.0)
    g = cot[...]
    normed, inv = normed_of(after_s[...])
    grad = gh2[...]
    small_out[0:1, :] = column_sum(grad * normed)
    small_out[1:2, :] = column_sum(grad)
    grad_after = g + norm_back(grad * vecs[1:2, :], normed, inv)
    after_out[...] = grad_after
    small_out[2:3, :] = column_sum(grad_after)
    small_out[3:4, :] = column_sum(g)
    small_out[4:8, :] = jnp.zeros((4, D), F32)
    half = grad_after.astype(BF)
    gow_out[...] = tn(att, half).astype(BF)
    gatt_out[...] = nt(half, out_w).astype(BF)


def back_kernel(slots, images, qk_w, vo_w, vecs, h1, qkv, pt, gatt, grad_after, cut, paste,
                out, gqk_out, gv_out, small_out, ds_out,
                rows, gw, gp, gpo):
    load_rows(images, rows, slots)
    wide = BLOCKS * WROWS
    for s in range(slots):
        gw[s * wide : (s + 1) * wide, :] = nn(
            cut[...], gatt[s * ROWS : (s + 1) * ROWS, :]
        ).astype(BF)
    half = head_masks(BF)
    full = head_masks(F32)
    ds_out[...] = jnp.zeros_like(ds_out)
    small_out[...] = jnp.zeros_like(small_out)

    def step(iw, carry):
        at = pl.ds(pl.multiple_of(iw * WROWS, WROWS), WROWS)
        for g in range(GROUPS):
            lanes = slice(g * GL, (g + 1) * GL)
            wide_lanes = slice(g * GS, (g + 1) * GS)
            qg = qkv[at, g * GL : (g + 1) * GL]
            kg = qkv[at, D + g * GL : D + (g + 1) * GL]
            vg = qkv[at, 2 * D + g * GL : 2 * D + (g + 1) * GL]
            dob = spread(gw[at, lanes], half)
            p = pt[iw, :, wide_lanes]
            dv = nn(p.astype(BF), dob)
            dp = nt(vg, dob)
            t = p * dp
            ds = t - p * jnp.sum(t, 0, keepdims=True)
            ds_out[:, wide_lanes] += ds
            dsh = ds.astype(BF)
            dk = nn(dsh, spread(qg, half))
            dq = diagonal(tn(dsh, kg), full) * SCALE
            gp[at, g * GL : (g + 1) * GL] = dq.astype(BF)
            gp[at, D + g * GL : D + (g + 1) * GL] = dk.astype(BF)
            gp[at, 2 * D + g * GL : 2 * D + (g + 1) * GL] = dv.astype(BF)
            small_out[2:3, lanes] += column_sum(dq)
            small_out[3:4, lanes] += column_sum(dv)
        return carry

    lax.fori_loop(0, slots * BLOCKS, step, 0)
    for s in range(slots):
        gpo[s * ROWS : (s + 1) * ROWS, :] = nn(
            paste[...], gp[s * wide : (s + 1) * wide, :]
        ).astype(BF)
    h1t = h1[...].T
    gqk_out[...] = nn(h1t, gpo[:, : 2 * D]).astype(BF)
    gv_out[...] = nn(h1t, gpo[:, 2 * D :]).astype(BF)
    grad = nt(gpo[:, : 2 * D], qk_w[...]) + nt(gpo[:, 2 * D :], vo_w[:, :D])
    normed, inv = normed_of(rows[...])
    small_out[0:1, :] = column_sum(grad * normed)
    small_out[1:2, :] = column_sum(grad)
    result = grad_after[...] + norm_back(grad * vecs[0:1, :], normed, inv)
    for s in range(slots):
        out[s] = result[s * ROWS : s * ROWS + TOK, :]


def call(kernel, outs, scratch, args, scalars=0, flops=0):
    vmem = pl.BlockSpec(memory_space=pltpu.VMEM)
    smem = pl.BlockSpec(memory_space=pltpu.SMEM)
    return pl.pallas_call(
        kernel,
        out_shape=[jax.ShapeDtypeStruct(s, t) for s, t in outs],
        in_specs=[smem] * scalars + [vmem] * (len(args) - scalars),
        out_specs=[vmem] * len(outs),
        scratch_shapes=[pltpu.VMEM(s, t) for s, t in scratch],
        compiler_params=pltpu.CompilerParams(vmem_limit_bytes=60 * 1024 * 1024),
        cost_estimate=pl.CostEstimate(flops=flops, bytes_accessed=8 << 20, transcendentals=0),
    )(*args)


def body(
    exchange,
    images,
    cotangent,
    image_counts,
    relative_index,
    region_labels,
    gain_first,
    shift_first,
    attend_weight,
    query_bias,
    value_bias,
    position_table,
    output_weight,
    output_bias,
    gain_second,
    shift_second,
    expand_weight,
    expand_bias,
    reduce_weight,
    reduce_bias,
):
    n = exchange.n
    slots = images.shape[0]
    small_in = (gain_first, shift_first, query_bias, value_bias, output_bias, gain_second,
                shift_second, reduce_bias, expand_bias, position_table)
    widths = [v.shape[0] for v in small_in]
    starts = np.concatenate([[0], np.cumsum(widths)]).tolist()
    padded = -(-starts[-1] // 128) * 128
    small = jnp.pad(jnp.concatenate(small_in), (0, padded - starts[-1])).reshape(1, padded)
    small = exchange.gather(small, 0)

    attend = attend_weight.reshape(-1, 3 * D)
    out_w = output_weight.reshape(-1, D)
    qk_w = exchange.gather(attend[:, : 2 * D], 0)
    vo_w = exchange.gather(jnp.concatenate([attend[:, 2 * D :], out_w], axis=1), 1)
    expand = exchange.gather(expand_weight.reshape(-1, FF), 0)
    reduce = exchange.gather(reduce_weight.reshape(-1, D), 1)

    vec = [small[:, a:b].reshape(-1) for a, b in zip(starts[:-1], starts[1:])]
    first = jnp.stack(vec[:4]).astype(F32)
    second = jnp.stack(vec[4:8]).astype(F32)
    ebias = vec[8].astype(F32).reshape(1, FF)
    table = vec[9][: TABLE_ROWS * HEADS].reshape(TABLE_ROWS, HEADS)
    onehot = (
        relative_index[:, :, None] == jnp.arange(TABLE_ROWS, dtype=jnp.int32)
    ).astype(F32)
    gap = WROWS - AREA
    bias = jnp.einsum("ijt,th->jhi", onehot.astype(BF), table, preferred_element_type=F32)
    bias = jnp.pad(bias, ((0, gap), (0, 0), (0, gap))).reshape(WROWS, HEADS * WROWS)
    side = SIDE // WIN
    labels = region_labels.reshape(side, WIN, side, WIN).transpose(0, 2, 1, 3).reshape(BLOCKS, AREA)
    allowed = (labels[:, :, None] == labels[:, None, :]).astype(F32)
    allowed = jnp.pad(allowed, ((0, 0), (0, gap), (0, gap)))
    cut_np = window_matrix()
    cut = jnp.asarray(cut_np, BF)
    paste = jnp.asarray(cut_np.T, BF)
    total_rows = slots * ROWS
    window_rows = slots * BLOCKS * WROWS

    qkv, pt, attended, h1 = call(
        functools.partial(attend_kernel, slots),
        [((window_rows, 3 * D), BF), ((slots * BLOCKS, WROWS, HEADS * WROWS), F32),
         ((total_rows, D), BF), ((total_rows, D), BF)],
        [((total_rows, D), F32), ((window_rows, D), BF)],
        (images, qk_w, vo_w, first, bias, allowed, cut, paste),
        flops=3 * 10**9,
    )
    (block_output, grad_after, gatt, g_out_w, g_expand, g_reduce, small_b, g_ebias) = call(
        functools.partial(mixer_kernel, slots),
        [((slots, TOK, D), F32), ((total_rows, D), F32), ((total_rows, D), BF), ((D, D), BF),
         ((D, FF), BF), ((FF, D), BF), ((8, D), F32), ((1, FF), F32)],
        [((total_rows, D), F32)] * 5 + [((total_rows, D), BF), ((D, total_rows), BF)],
        (image_counts, images, cotangent, attended, vo_w, expand, reduce, second, ebias),
        scalars=1,
        flops=6 * 10**9,
    )
    s_expand = exchange.scatter_sum(g_expand, 0, BF)
    s_reduce = exchange.scatter_sum(g_reduce, 1, BF)
    input_gradient, g_qk, g_v, small_a, ds = call(
        functools.partial(back_kernel, slots),
        [((slots, TOK, D), F32), ((D, 2 * D), BF), ((D, D), BF), ((8, D), F32),
         ((WROWS, HEADS * WROWS), F32)],
        [((total_rows, D), F32), ((window_rows, D), BF), ((window_rows, 3 * D), BF),
         ((total_rows, 3 * D), BF)],
        (images, qk_w, vo_w, first, h1, qkv, pt, gatt, grad_after, cut, paste),
        flops=5 * 10**9,
    )
    s_qk = exchange.scatter_sum(g_qk, 0, BF)
    s_vo = exchange.scatter_sum(jnp.concatenate([g_v, g_out_w], axis=1), 1, BF)

    ds = ds.reshape(WROWS, HEADS, WROWS)[:AREA, :, :AREA]
    g_table = jnp.einsum("ijt,jhi->th", onehot, ds, precision=lax.Precision.HIGHEST).reshape(-1)
    g_table = jnp.pad(g_table, (0, n * widths[9] - g_table.shape[0]))
    grads = (small_a[0], small_a[1], small_a[2], small_a[3], small_b[2], small_b[0], small_b[1],
             small_b[3], g_ebias[0], g_table)
    packed = jnp.concatenate([g.reshape(n, -1) for g in grads], axis=1)
    packed = jnp.pad(packed, ((0, 0), (0, padded - starts[-1])))
    mine = exchange.scatter_sum(packed, 0, F32)[0]
    own = [mine[a:b] for a, b in zip(starts[:-1], starts[1:])]
    g_attend = jnp.concatenate([s_qk, s_vo[:, :D]], axis=1).reshape(-1)
    return (
        block_output, input_gradient, own[0], own[1], g_attend, own[2], own[3], own[9],
        s_vo[:, D:].reshape(-1), own[4], own[5], own[6], s_expand.reshape(-1), own[8],
        s_reduce.reshape(-1), own[7],
    )


def solution(mesh):
    exchange = Exchange(mesh)
    split = P("dev", None, None)
    flat = P("dev")
    return jax.shard_map(
        functools.partial(body, exchange),
        mesh=mesh,
        in_specs=(split, split, flat, P(), P()) + (flat,) * 14,
        out_specs=(split, split) + (flat,) * 14,
        check_vma=False,
    )
```
